32 devices in a mesh: gx: 8 (over z, y), gy: 4 (over x, core).
Axes of the slice: x: 2, y: 2, z: 4, core: 2. Of those that a mesh axis runs over, the one named last changes fastest.
Arguments:
- velocity: float32 [3, 64, 32, 128], P(None, 'gx', 'gy'), may hold values from -6 to 6
- surfaces: float32 [8, 6, 64, 32, 128], P(None, None, 'gx', 'gy'), may hold values from -2 to 2
- mean_stress: float32 [64, 32, 128], P('gx', 'gy'), may hold values from -6 to 6
- zone: int32 [64, 32, 128], P('gx', 'gy'), may hold values from 0 to 7
- sponge: int32 [64, 32, 128], P('gx', 'gy'), may hold values from 0 to 3
- moduli: float32 [8, 3], replicated, may hold values from 0.5 to 2
- yields: float32 [8, 8], replicated, may hold values from 0.05 to 1
Outputs:
- new_velocity: float32 [3, 64, 32, 128], P(None, 'gx', 'gy')
- new_stress: float32 [6, 64, 32, 128], P(None, 'gx', 'gy')
The draws below stay inside these ranges and needn't reach their ends.
All inputs are finite; a program needn't handle non-finite values.
Results may differ from the reference program's by a relative error of at most 0.0001.
Values sent between devices are 32-bit elements; how exact they have to be, the bound alone decides.
A program may use at most 64 MiB of HBM per device.

```python
import math
import jax
import jax.numpy as jnp
from jax import lax

NZ = 128
ITERS = 3
SURF = 8
ZONES = 8
NX = 64
NY = 32


def plant(values, key, low, high):
    longest = values.shape.index(max(values.shape))
    spots = []
    for shift in (0, 1):
        where = [jax.random.randint(jax.random.fold_in(key, axis), (), 0, length) for axis, length in enumerate(values.shape)]
        where[longest] = (where[longest] + shift) % values.shape[longest]
        spots.append(tuple(where))
    return values.at[spots[0]].set(low).at[spots[1]].set(high)


def block_levels(stream_key, shape, pieces, least, largest):
    level, own = 1.0, jax.random.fold_in(stream_key, 6)
    for axis_at, shards_of in pieces:
        steps = jnp.exp(jax.random.uniform(jax.random.fold_in(own, axis_at), (shards_of,), jnp.float32, least / len(pieces), largest / len(pieces)))
        level = level * jnp.repeat(steps, shape[axis_at] // shards_of).reshape([-1 if axis == axis_at else 1 for axis in range(len(shape))])
    return level


def gaussian(stream_key, shape, spread, bound, pieces=(), kind=jnp.bfloat16):
    level = block_levels(stream_key, shape, pieces, -0.22, 0.18) if pieces else 1.0
    entries = jax.random.normal(stream_key, shape, jnp.float32) * spread * level
    return jnp.minimum(jnp.maximum(entries, -bound), bound).astype(kind)


def setup_inputs(seed: int = 0) -> dict:
    seeds = jax.random.split(jax.random.key(seed), 8)
    return {
        "velocity": gaussian(seeds[0], (3, NX, NY, NZ), 1.0, 6.0, ((1, 8), (2, 4)), jnp.float32),
        "surfaces": gaussian(seeds[1], (SURF, 6, NX, NY, NZ), 0.3, 2.0, ((2, 8), (3, 4)), jnp.float32),
        "mean_stress": gaussian(seeds[2], (NX, NY, NZ), 1.0, 6.0, ((0, 8), (1, 4)), jnp.float32),
        "zone": plant(jax.random.randint(seeds[3], (NX, NY, NZ), 0, ZONES), jax.random.fold_in(seeds[3], 1), 0, ZONES - 1).astype(jnp.int32),
        "sponge": plant(jax.random.randint(seeds[4], (NX, NY, NZ), 0, 4), jax.random.fold_in(seeds[4], 1), 0, 3).astype(jnp.int32),
        "moduli": jnp.clip(jnp.exp(jax.random.uniform(seeds[5], (ZONES, 3), jnp.float32, math.log(0.5), math.log(2.0))), 0.5, 2.0),
        "yields": jnp.clip(jnp.exp(jax.random.uniform(seeds[6], (ZONES, SURF), jnp.float32, math.log(0.05), math.log(1.0))), 0.05, 1.0),
    }


coef_near = 9.0 / 8.0
coef_far = -1.0 / 24.0
time_step = 0.1
sponge_rate = 0.1

def shifted(field, axis_pos, offset):
    lead = field.ndim - 3
    slices = [slice(None)] * lead
    for position in range(3):
        length = field.shape[lead + position]
        if position == axis_pos:
            slices.append(slice(2 + offset, length - 2 + offset))
        else:
            slices.append(slice(2, length - 2))
    return field[tuple(slices)]

def forward(field, axis_pos):
    return coef_near * (shifted(field, axis_pos, 1) - shifted(field, axis_pos, 0)) + coef_far * (shifted(field, axis_pos, 2) - shifted(field, axis_pos, -1))

def backward(field, axis_pos):
    return coef_near * (shifted(field, axis_pos, 0) - shifted(field, axis_pos, -1)) + coef_far * (shifted(field, axis_pos, 1) - shifted(field, axis_pos, -2))

def lookup(table, zone):
    result = jnp.zeros((table.shape[1],) + zone.shape, table.dtype)
    for index_zone in range(table.shape[0]):
        picked = (zone == index_zone)[None]
        result = result + jnp.where(picked, table[index_zone][:, None, None, None], jnp.zeros((), table.dtype))
    return result

def total_stress(surfaces, mean_stress):
    diagonal_mask = jnp.array([1.0, 1.0, 1.0, 0.0, 0.0, 0.0], dtype=jnp.float32)[:, None, None, None]
    return lax.optimization_barrier(jnp.sum(surfaces, axis=0)) + diagonal_mask * mean_stress[None]

def advance(velocity, stress_pad, buoyancy, damping):
    accel = jnp.stack([forward(stress_pad[0], 0) + backward(stress_pad[3], 1) + backward(stress_pad[4], 2), backward(stress_pad[3], 0) + forward(stress_pad[1], 1) + backward(stress_pad[5], 2), backward(stress_pad[4], 0) + backward(stress_pad[5], 1) + forward(stress_pad[2], 2)])
    return (velocity + time_step * buoyancy[None] * accel) * damping[None]

def plastic(surfaces, mean_stress, velocity_pad, bulk, shear, limit):
    rate_xx = backward(velocity_pad[0], 0)
    rate_yy = backward(velocity_pad[1], 1)
    rate_zz = backward(velocity_pad[2], 2)
    rate_xy = 0.5 * (forward(velocity_pad[0], 1) + forward(velocity_pad[1], 0))
    rate_xz = 0.5 * (forward(velocity_pad[0], 2) + forward(velocity_pad[2], 0))
    rate_yz = 0.5 * (forward(velocity_pad[1], 2) + forward(velocity_pad[2], 1))
    trace = rate_xx + rate_yy + rate_zz
    mean_stress = mean_stress + time_step * bulk * trace
    third = trace / 3.0
    deviator = jnp.stack([rate_xx - third, rate_yy - third, rate_zz - third, rate_xy, rate_xz, rate_yz])
    trial = surfaces + 2.0 * time_step / 8.0 * shear[None, None] * deviator[None]
    magnitude = jnp.sqrt(0.5 * lax.optimization_barrier(jnp.sum(trial[:, :3] * trial[:, :3], axis=1)) + lax.optimization_barrier(jnp.sum(trial[:, 3:] * trial[:, 3:], axis=1)))
    factor = limit / jnp.maximum(magnitude, limit)
    surfaces = trial * factor[:, None]
    return (surfaces, mean_stress, total_stress(surfaces, mean_stress))

def pad_all(field):
    return jnp.pad(field, [(0, 0)] * (field.ndim - 3) + [(2, 2)] * 3)

def reference(velocity, surfaces, mean_stress, zone, sponge, moduli, yields):
    material = lookup(moduli, zone)
    bulk, shear, buoyancy = (material[0], material[1], material[2])
    limit = lookup(yields, zone)
    damping = 1.0 - sponge_rate * sponge.astype(jnp.float32)
    stress = total_stress(surfaces, mean_stress)
    for turn_index in range(ITERS):
        velocity = advance(velocity, pad_all(stress), buoyancy, damping)
        surfaces, mean_stress, stress = plastic(surfaces, mean_stress, pad_all(velocity), bulk, shear, limit)
    return (velocity, stress)
```

```python
import functools

import jax
import jax.numpy as jnp
from jax import lax
from jax.experimental import pallas as pl
from jax.experimental.pallas import tpu as pltpu
from jax.sharding import PartitionSpec as P

ITERS = 3
SURF = 8
ZONES = 8
C1 = 9.0 / 8.0
C2 = -1.0 / 24.0
DT = 0.1
SPONGE = 0.1

B = 8
WX = 12
WY = 16
XX, YY, ZZ, XY, XZ, YZ = range(6)

NORMAL = ((XX, XY, XZ), (YY, XY, YZ))
ALONG = ((XY, YY, YZ), (XY, XX, XZ))
VELOCITY = ((0, 1, 2), (1, 0, 2))

FACES = ((0, -1), (0, 1), (1, -1), (1, 1))
CORNERS = ((-1, -1), (-1, 1), (1, -1), (1, 1))


def kernel(
    nx, ny,
    velocity, surfaces, mean_in, zone, sponge, moduli, yields,
    velocity_out, stress_out,
    surf, mean, S, V, A, D, bulk, shear, limit, strips,
    face_out, face_in, corner_out, corner_in,
    load_sem, face_send, face_recv, corner_send, corner_recv,
):
    px, py = lax.axis_index("gx"), lax.axis_index("gy")
    f32 = jnp.float32

    load_surf = pltpu.make_async_copy(surfaces, surf, load_sem.at[0])
    load_surf.start()

    def has(axis, side):
        at, count = ((px, nx), (py, ny))[axis]
        return at > 0 if side < 0 else at < count - 1

    def has_corner(dx, dy):
        return jnp.logical_and(has(0, dx), has(1, dy))

    def device(dx, dy):
        return (px + dx, py + dy)

    barrier = pltpu.get_barrier_semaphore()
    neighbours = [((dx, 0), has(0, dx)) for dx in (-1, 1)]
    neighbours += [((0, dy), has(1, dy)) for dy in (-1, 1)]
    neighbours += [(d, has_corner(*d)) for d in CORNERS]
    for (dx, dy), there in neighbours:
        @pl.when(there)
        def _():
            pl.semaphore_signal(
                barrier, inc=1, device_id=device(dx, dy),
                device_id_type=pl.DeviceIdType.MESH,
            )

    zero = jnp.zeros((B, 128), f32)

    for axis, side in FACES:
        @pl.when(jnp.logical_not(has(axis, side)))
        def _():
            for t in range(ITERS):
                for tile in range(11):
                    face_in[t, axis, (side + 1) // 2, tile] = zero
    for index, (dx, dy) in enumerate(CORNERS):
        @pl.when(jnp.logical_not(has_corner(dx, dy)))
        def _():
            for t in range(ITERS):
                for part in range(3):
                    corner_in[t, index, part * 8:part * 8 + 8, :] = zero

    @pl.loop(0, 6 * WX)
    def _(i):
        S[i, 0:8, :] = zero
        S[i, 8:16, :] = zero

    @pl.loop(0, 24)
    def _(i):
        strips[i, 0:8, :] = zero
        strips[i, 8:16, :] = zero

    def pick(table, column, b0, b1, b2):
        v = [table[z, column] for z in range(ZONES)]
        a = [jnp.where(b0, v[2 * n + 1], v[2 * n]) for n in range(4)]
        c = [jnp.where(b1, a[2 * n + 1], a[2 * n]) for n in range(2)]
        return jnp.where(b2, c[1], c[0])

    @pl.loop(0, B)
    def _(i):
        z = zone[i]
        b0, b1, b2 = (z & 1) > 0, (z & 2) > 0, (z & 4) > 0
        damping = 1.0 - SPONGE * sponge[i].astype(f32)
        bulk[i] = DT * pick(moduli, 0, b0, b1, b2)
        shear[i] = (2.0 * DT / SURF) * pick(moduli, 1, b0, b1, b2)
        A[i] = DT * pick(moduli, 2, b0, b1, b2) * damping
        D[i] = damping
        for k in range(SURF):
            limit[k, i] = pick(yields, k, b0, b1, b2)
        mean[i] = mean_in[i]
        for c in range(3):
            V[c * WX + 2 + i, 4:12, :] = velocity[c, i]

    lane = lax.broadcasted_iota(jnp.int32, (B, 128), 1)

    def mask(keep, value):
        return jnp.where(keep, f32(value), f32(0))

    f_up1 = mask(lane < 127, C1)
    f_up2 = mask(lane < 126, C2)
    f_dn1 = mask(lane >= 1, C2)
    b_dn1 = mask(lane >= 1, C1)
    b_up1 = mask(lane < 127, C2)
    b_dn2 = mask(lane >= 2, C2)

    def forward_z(f):
        return (
            f_up1 * pltpu.roll(f, 127, 1) - C1 * f
            + f_up2 * pltpu.roll(f, 126, 1) - f_dn1 * pltpu.roll(f, 1, 1)
        )

    def backward_z(f):
        return (
            C1 * f - b_dn1 * pltpu.roll(f, 1, 1)
            + b_up1 * pltpu.roll(f, 127, 1) - b_dn2 * pltpu.roll(f, 2, 1)
        )

    def forward_of(at):
        return C1 * (at(1) - at(0)) + C2 * (at(2) - at(-1))

    def backward_of(at):
        return C1 * (at(0) - at(-1)) + C2 * (at(1) - at(-2))

    def along_x(ref, c, i):
        return lambda o: ref[c * WX + 2 + i + o, 4:12, :]

    def along_rows(ref, n):
        return lambda o: ref[n, 4 + o:12 + o, :]

    def along_y(ref, c, i):
        return along_rows(ref, c * WX + 2 + i)

    S_rows = S.reshape(6 * WX * WY, 128)
    V_rows = V.reshape(3 * WX * WY, 128)
    A_rows = A.reshape(B * B, 128)

    def rows_of(c, k):
        return (pl.ds((c * WX + 2) * WY + 4 + k, B, stride=WY), slice(None))

    def get_s(axis, c, k):
        return S[c * WX + 2 + k, 4:12, :] if axis == 0 else S_rows[rows_of(c, k)]

    def get_v(axis, c, k):
        return V[c * WX + 2 + k, 4:12, :] if axis == 0 else V_rows[rows_of(c, k)]

    def set_v(axis, c, k, value):
        if axis == 0:
            V[c * WX + 2 + k, 4:12, :] = value
        else:
            V_rows[rows_of(c, k)] = value

    def get_a(axis, k):
        return A[k] if axis == 0 else A_rows[pl.ds(k, B, stride=B), :]

    def face_copy(t, axis, side, toward):
        own, other = (side + 1) // 2, (1 - side) // 2
        tiles = pl.ds(0, 11 if t == 0 else 9)
        shift = (toward, 0) if axis == 0 else (0, toward)
        return pltpu.make_async_remote_copy(
            src_ref=face_out.at[t, axis, own, tiles],
            dst_ref=face_in.at[t, axis, other, tiles],
            send_sem=face_send.at[t, axis, own],
            recv_sem=face_recv.at[t, axis, other],
            device_id=device(*shift),
            device_id_type=pl.DeviceIdType.MESH,
        )

    def corner_copy(t, index, toward):
        dx, dy = CORNERS[toward]
        return pltpu.make_async_remote_copy(
            src_ref=corner_out.at[t, index],
            dst_ref=corner_in.at[t, 3 - index],
            send_sem=corner_send.at[t, index],
            recv_sem=corner_recv.at[t, 3 - index],
            device_id=device(dx, dy),
            device_id_type=pl.DeviceIdType.MESH,
        )

    def send_corners(t):
        for index, (dx, dy) in enumerate(CORNERS):
            kx, ky = (6 if dx > 0 else 0), (6 if dy > 0 else 0)
            for n in range(3):
                for k in range(2):
                    row = (n * 2 + k) * 2
                    corner_out[t, index, row:row + 2, :] = S[
                        ALONG[0][n] * WX + 2 + kx + k, 4 + ky:6 + ky, :
                    ]
                    for m in range(2):
                        corner_out[t, index, 12 + row + m:13 + row + m, :] = S[
                            ALONG[1][n] * WX + 2 + kx + m, 4 + ky + k:5 + ky + k, :
                        ]

            @pl.when(has_corner(dx, dy))
            def _():
                corner_copy(t, index, index).start()

    def send_faces(t):
        for axis, side in FACES:
            n, tg, z = NORMAL[axis]
            vn, vt, vz = VELOCITY[axis]
            s = functools.partial(get_s, axis)
            v = functools.partial(get_v, axis)
            if side > 0:
                tiles = [s(n, 7), s(tg, 6), s(tg, 7), s(z, 6), s(z, 7),
                         v(vn, 6), v(vn, 7), v(vt, 7), v(vz, 7)]
                a_from = 6
            else:
                tiles = [s(n, 0), s(n, 1), s(tg, 0), s(z, 0),
                         v(vn, 0), v(vt, 0), v(vt, 1), v(vz, 0), v(vz, 1)]
                a_from = 0
            if t == 0:
                tiles += [get_a(axis, a_from), get_a(axis, a_from + 1)]
            for index, tile in enumerate(tiles):
                face_out[t, axis, (side + 1) // 2, index] = tile

            @pl.when(has(axis, side))
            def _():
                face_copy(t, axis, side, side).start()

    def partial_velocity():
        @pl.loop(0, B)
        def _(i):
            sx = functools.partial(along_x, S)
            sy = functools.partial(along_y, S)
            here = lambda c: S[c * WX + 2 + i, 4:12, :]
            accel = (
                forward_of(sx(XX, i)) + backward_of(sy(XY, i)) + backward_z(here(XZ)),
                backward_of(sx(XY, i)) + forward_of(sy(YY, i)) + backward_z(here(YZ)),
                backward_of(sx(XZ, i)) + backward_of(sy(YZ, i)) + forward_z(here(ZZ)),
            )
            for c in range(3):
                V[c * WX + 2 + i, 4:12, :] = (
                    D[i] * V[c * WX + 2 + i, 4:12, :] + A[i] * accel[c]
                )

    def receive(t):
        for axis, side in FACES:
            @pl.when(has(axis, side))
            def _():
                face_copy(t, axis, -side, side).wait_recv()
        for index, (dx, dy) in enumerate(CORNERS):
            @pl.when(has_corner(dx, dy))
            def _():
                corner_copy(t, 3 - index, index).wait_recv()

    def finish_velocity(t):
        for index, (dx, dy) in enumerate(CORNERS):
            for axis, side, other in ((0, dx, dy), (1, dy, dx)):
                at = 2 if other < 0 else 12
                for n in range(6):
                    row = axis * 12 + n * 2
                    strips[(axis * 2 + (side + 1) // 2) * 6 + n, at:at + 2, :] = (
                        corner_in[t, index, row:row + 2, :]
                    )
        for axis in range(2):
            n, tg, z = NORMAL[axis]
            vn, vt, vz = VELOCITY[axis]
            s = functools.partial(get_s, axis)
            a = functools.partial(get_a, axis)

            def add(c, k, value):
                set_v(axis, c, k, get_v(axis, c, k) + a(k) * value)

            def strip(side, m, k):
                return along_rows(strips, (axis * 2 + side) * 6 + m * 2 + k)

            lo = lambda m: face_in[t, axis, 0, m]
            hi = lambda m: face_in[t, axis, 1, m]
            a_lo = lambda k: face_in[0, axis, 0, 9 + k]
            a_hi = lambda k: face_in[0, axis, 1, 9 + k]

            set_v(axis, vn, -2, lo(5) + a_lo(0) * (
                C2 * s(n, 0) + backward_of(strip(0, 0, 0))))
            set_v(axis, vn, -1, lo(6) + a_lo(1) * (
                C1 * s(n, 0) + C2 * s(n, 1) + backward_of(strip(0, 0, 1))))
            set_v(axis, vt, -1, lo(7) + a_lo(1) * (
                C2 * s(tg, 0) + forward_of(strip(0, 1, 1))))
            set_v(axis, vz, -1, lo(8) + a_lo(1) * (
                C2 * s(z, 0) + backward_of(strip(0, 2, 1))))
            set_v(axis, vn, 8, hi(4) + a_hi(0) * (
                -C2 * s(n, 7) + backward_of(strip(1, 0, 0))))
            set_v(axis, vt, 8, hi(5) + a_hi(0) * (
                -C1 * s(tg, 7) - C2 * s(tg, 6) + forward_of(strip(1, 1, 0))))
            set_v(axis, vt, 9, hi(6) + a_hi(1) * (
                -C2 * s(tg, 7) + forward_of(strip(1, 1, 1))))
            set_v(axis, vz, 8, hi(7) + a_hi(0) * (
                -C1 * s(z, 7) - C2 * s(z, 6) + backward_of(strip(1, 2, 0))))
            set_v(axis, vz, 9, hi(8) + a_hi(1) * (
                -C2 * s(z, 7) + backward_of(strip(1, 2, 1))))

            add(vn, 0, -C2 * lo(0))
            add(vn, 6, C2 * hi(0))
            add(vn, 7, C1 * hi(0) + C2 * hi(1))
            for c, m, h in ((vt, 1, 2), (vz, 3, 3)):
                add(c, 0, -C1 * lo(m + 1) - C2 * lo(m))
                add(c, 1, -C2 * lo(m + 1))
                add(c, 7, C2 * hi(h))

    def plastic():
        @pl.loop(0, B)
        def _(i):
            vx = functools.partial(along_x, V)
            vy = functools.partial(along_y, V)
            here = lambda c: V[c * WX + 2 + i, 4:12, :]
            xx = backward_of(vx(0, i))
            yy = backward_of(vy(1, i))
            zz = backward_z(here(2))
            trace = xx + yy + zz
            third = trace * (1.0 / 3.0)
            g = shear[i]
            h = 0.5 * g
            move = (
                g * (xx - third), g * (yy - third), g * (zz - third),
                h * (forward_of(vy(0, i)) + forward_of(vx(1, i))),
                h * (forward_z(here(0)) + forward_of(vx(2, i))),
                h * (forward_z(here(1)) + forward_of(vy(2, i))),
            )
            pressure = mean[i] + bulk[i] * trace
            mean[i] = pressure
            total = [None] * 6
            for k in range(SURF):
                trial = [surf[k, c, i] + move[c] for c in range(6)]
                sq = [f * f for f in trial]
                size2 = 0.5 * (sq[0] + sq[1] + sq[2]) + (sq[3] + sq[4] + sq[5])
                lim = limit[k, i]
                factor = lim * lax.rsqrt(jnp.maximum(size2, lim * lim))
                for c in range(6):
                    new = trial[c] * factor
                    surf[k, c, i] = new
                    total[c] = new if k == 0 else total[c] + new
            for c in range(6):
                S[c * WX + 2 + i, 4:12, :] = total[c] + pressure if c < 3 else total[c]

    load_surf.wait()

    @pl.loop(0, B)
    def _(i):
        for c in range(6):
            total = surf[0, c, i]
            for k in range(1, SURF):
                total = total + surf[k, c, i]
            S[c * WX + 2 + i, 4:12, :] = total + mean[i] if c < 3 else total

    count = sum(there.astype(jnp.int32) for _, there in neighbours)
    pl.semaphore_wait(barrier, count)

    for t in range(ITERS):
        send_corners(t)
        partial_velocity()
        send_faces(t)
        receive(t)
        finish_velocity(t)
        plastic()

    for c in range(3):
        for i in range(B):
            velocity_out[c, i] = V[c * WX + 2 + i, 4:12, :]
    for c in range(6):
        for i in range(B):
            stress_out[c, i] = S[c * WX + 2 + i, 4:12, :]

    for t in range(ITERS):
        for axis, side in FACES:
            @pl.when(has(axis, side))
            def _():
                face_copy(t, axis, side, side).wait_send()
        for index, (dx, dy) in enumerate(CORNERS):
            @pl.when(has_corner(dx, dy))
            def _():
                corner_copy(t, index, index).wait_send()


def body(nx, ny, velocity, surfaces, mean_stress, zone, sponge, moduli, yields):
    vmem = pl.BlockSpec(memory_space=pltpu.VMEM)
    smem = pl.BlockSpec(memory_space=pltpu.SMEM)
    f32 = jnp.float32
    tiles = lambda *lead: pltpu.VMEM(lead + (B, 128), f32)
    return pl.pallas_call(
        functools.partial(kernel, nx, ny),
        out_shape=(
            jax.ShapeDtypeStruct((3, B, B, 128), f32),
            jax.ShapeDtypeStruct((6, B, B, 128), f32),
        ),
        in_specs=[vmem, pl.BlockSpec(memory_space=pl.ANY), vmem, vmem, vmem, smem, smem],
        out_specs=(vmem, vmem),
        scratch_shapes=[
            tiles(SURF, 6, B),
            tiles(B),
            pltpu.VMEM((6 * WX, WY, 128), f32),
            pltpu.VMEM((3 * WX, WY, 128), f32),
            tiles(B), tiles(B), tiles(B), tiles(B),
            tiles(SURF, B),
            pltpu.VMEM((24, WY, 128), f32),
            tiles(ITERS, 2, 2, 11),
            tiles(ITERS, 2, 2, 11),
            pltpu.VMEM((ITERS, 4, 24, 128), f32),
            pltpu.VMEM((ITERS, 4, 24, 128), f32),
            pltpu.SemaphoreType.DMA((1,)),
            pltpu.SemaphoreType.DMA((ITERS, 2, 2)),
            pltpu.SemaphoreType.DMA((ITERS, 2, 2)),
            pltpu.SemaphoreType.DMA((ITERS, 4)),
            pltpu.SemaphoreType.DMA((ITERS, 4)),
        ],
        compiler_params=pltpu.CompilerParams(
            collective_id=0, has_side_effects=True, vmem_limit_bytes=32 << 20
        ),
    )(velocity, surfaces, mean_stress, zone, sponge, moduli, yields)


def solution(mesh):
    return jax.shard_map(
        functools.partial(body, mesh.shape["gx"], mesh.shape["gy"]),
        mesh=mesh,
        in_specs=(
            P(None, "gx", "gy", None),
            P(None, None, "gx", "gy", None),
            P("gx", "gy", None),
            P("gx", "gy", None),
            P("gx", "gy", None),
            P(),
            P(),
        ),
        out_specs=(P(None, "gx", "gy", None), P(None, "gx", "gy", None)),
        check_vma=False,
    )
```

```python
import functools

import jax
import jax.numpy as jnp
from jax import lax
from jax.experimental import pallas as pl
from jax.experimental.pallas import tpu as pltpu
from jax.sharding import PartitionSpec as P

ITERS = 3
SURF = 8
ZONES = 8
C1 = 9.0 / 8.0
C2 = -1.0 / 24.0
DT = 0.1
SPONGE = 0.1

B = 8
WX = 12
WY = 16
XX, YY, ZZ, XY, XZ, YZ = range(6)

NORMAL = ((XX, XY, XZ), (YY, XY, YZ))
ALONG = ((XY, YY, YZ), (XY, XX, XZ))
VELOCITY = ((0, 1, 2), (1, 0, 2))

FACES = ((0, -1), (0, 1), (1, -1), (1, 1))
CORNERS = ((-1, -1), (-1, 1), (1, -1), (1, 1))


def kernel(
    nx, ny,
    velocity_hbm, surfaces, mean_hbm, zone_hbm, sponge_hbm, moduli_hbm, yields_hbm,
    velocity_out, stress_out,
    velocity, zone, sponge, moduli, yields, surf, mean, S, V, A, D, bulk, shear, limit, strips,
    face_out, face_in, corner_out, corner_in,
    load_sem, face_send, face_recv, corner_send, corner_recv,
):
    px, py = lax.axis_index("gx"), lax.axis_index("gy")
    f32 = jnp.float32

    small = (
        (moduli_hbm, moduli), (yields_hbm, yields), (zone_hbm, zone),
        (sponge_hbm, sponge), (mean_hbm, mean), (velocity_hbm, velocity),
    )
    loads = [
        pltpu.make_async_copy(source, target, load_sem.at[index])
        for index, (source, target) in enumerate(small)
    ]
    surface_loads = [
        pltpu.make_async_copy(surfaces.at[k], surf.at[k], load_sem.at[len(small) + k])
        for k in range(SURF)
    ]
    for load in loads + surface_loads:
        load.start()

    def has(axis, side):
        at, count = ((px, nx), (py, ny))[axis]
        return at > 0 if side < 0 else at < count - 1

    def has_corner(dx, dy):
        return jnp.logical_and(has(0, dx), has(1, dy))

    def device(dx, dy):
        return (px + dx, py + dy)

    barrier = pltpu.get_barrier_semaphore()
    neighbours = [((dx, 0), has(0, dx)) for dx in (-1, 1)]
    neighbours += [((0, dy), has(1, dy)) for dy in (-1, 1)]
    neighbours += [(d, has_corner(*d)) for d in CORNERS]
    for (dx, dy), there in neighbours:
        @pl.when(there)
        def _():
            pl.semaphore_signal(
                barrier, inc=1, device_id=device(dx, dy),
                device_id_type=pl.DeviceIdType.MESH,
            )

    zero = jnp.zeros((B, 128), f32)

    for axis, side in FACES:
        @pl.when(jnp.logical_not(has(axis, side)))
        def _():
            for t in range(ITERS):
                for tile in range(11):
                    face_in[t, axis, (side + 1) // 2, tile] = zero
    for index, (dx, dy) in enumerate(CORNERS):
        @pl.when(jnp.logical_not(has_corner(dx, dy)))
        def _():
            for t in range(ITERS):
                for part in range(3):
                    corner_in[t, index, part * 8:part * 8 + 8, :] = zero

    @pl.loop(0, 6 * WX)
    def _(i):
        S[i, 0:8, :] = zero
        S[i, 8:16, :] = zero

    @pl.loop(0, 24)
    def _(i):
        strips[i, 0:8, :] = zero
        strips[i, 8:16, :] = zero

    for load in loads:
        load.wait()

    modulus = lambda z, column: moduli[column, z]
    strength = lambda z, column: yields[z, column]

    def pick(table, column, b0, b1, b2):
        v = [table(z, column) for z in range(ZONES)]
        a = [jnp.where(b0, v[2 * n + 1], v[2 * n]) for n in range(4)]
        c = [jnp.where(b1, a[2 * n + 1], a[2 * n]) for n in range(2)]
        return jnp.where(b2, c[1], c[0])

    @pl.loop(0, B)
    def _(i):
        z = zone[i]
        b0, b1, b2 = (z & 1) > 0, (z & 2) > 0, (z & 4) > 0
        damping = 1.0 - SPONGE * sponge[i].astype(f32)
        bulk[i] = DT * pick(modulus, 0, b0, b1, b2)
        shear[i] = (2.0 * DT / SURF) * pick(modulus, 1, b0, b1, b2)
        A[i] = DT * pick(modulus, 2, b0, b1, b2) * damping
        D[i] = damping
        for k in range(SURF):
            limit[k, i] = pick(strength, k, b0, b1, b2)
        for c in range(3):
            V[c * WX + 2 + i, 4:12, :] = velocity[c, i]

    lane = lax.broadcasted_iota(jnp.int32, (B, 128), 1)

    def mask(keep, value):
        return jnp.where(keep, f32(value), f32(0))

    f_up1 = mask(lane < 127, C1)
    f_up2 = mask(lane < 126, C2)
    f_dn1 = mask(lane >= 1, C2)
    b_dn1 = mask(lane >= 1, C1)
    b_up1 = mask(lane < 127, C2)
    b_dn2 = mask(lane >= 2, C2)

    def forward_z(f):
        return (
            f_up1 * pltpu.roll(f, 127, 1) - C1 * f
            + f_up2 * pltpu.roll(f, 126, 1) - f_dn1 * pltpu.roll(f, 1, 1)
        )

    def backward_z(f):
        return (
            C1 * f - b_dn1 * pltpu.roll(f, 1, 1)
            + b_up1 * pltpu.roll(f, 127, 1) - b_dn2 * pltpu.roll(f, 2, 1)
        )

    def forward_of(at):
        return C1 * (at(1) - at(0)) + C2 * (at(2) - at(-1))

    def backward_of(at):
        return C1 * (at(0) - at(-1)) + C2 * (at(1) - at(-2))

    def along_x(ref, c, i):
        return lambda o: ref[c * WX + 2 + i + o, 4:12, :]

    def along_rows(ref, n):
        return lambda o: ref[n, 4 + o:12 + o, :]

    def along_y(ref, c, i):
        return along_rows(ref, c * WX + 2 + i)

    S_rows = S.reshape(6 * WX * WY, 128)
    V_rows = V.reshape(3 * WX * WY, 128)
    A_rows = A.reshape(B * B, 128)

    def rows_of(c, k):
        return (pl.ds((c * WX + 2) * WY + 4 + k, B, stride=WY), slice(None))

    def get_s(axis, c, k):
        return S[c * WX + 2 + k, 4:12, :] if axis == 0 else S_rows[rows_of(c, k)]

    def get_v(axis, c, k):
        return V[c * WX + 2 + k, 4:12, :] if axis == 0 else V_rows[rows_of(c, k)]

    def set_v(axis, c, k, value):
        if axis == 0:
            V[c * WX + 2 + k, 4:12, :] = value
        else:
            V_rows[rows_of(c, k)] = value

    def get_a(axis, k):
        return A[k] if axis == 0 else A_rows[pl.ds(k, B, stride=B), :]

    def face_copy(t, axis, side, toward, part):
        own, other = (side + 1) // 2, (1 - side) // 2
        split = 7 if side > 0 else 6
        start, stop = (2 if t else 0, split) if part == 0 else (split, 11)
        tiles = pl.ds(start, stop - start)
        shift = (toward, 0) if axis == 0 else (0, toward)
        return pltpu.make_async_remote_copy(
            src_ref=face_out.at[t, axis, own, tiles],
            dst_ref=face_in.at[t, axis, other, tiles],
            send_sem=face_send.at[t, axis, own, part],
            recv_sem=face_recv.at[t, axis, other, part],
            device_id=device(*shift),
            device_id_type=pl.DeviceIdType.MESH,
        )

    def corner_copy(t, index, toward):
        dx, dy = CORNERS[toward]
        return pltpu.make_async_remote_copy(
            src_ref=corner_out.at[t, index],
            dst_ref=corner_in.at[t, 3 - index],
            send_sem=corner_send.at[t, index],
            recv_sem=corner_recv.at[t, 3 - index],
            device_id=device(dx, dy),
            device_id_type=pl.DeviceIdType.MESH,
        )

    def send_corners(t):
        for index, (dx, dy) in enumerate(CORNERS):
            kx, ky = (6 if dx > 0 else 0), (6 if dy > 0 else 0)
            for n in range(3):
                for k in range(2):
                    row = (n * 2 + k) * 2
                    corner_out[t, index, row:row + 2, :] = S[
                        ALONG[0][n] * WX + 2 + kx + k, 4 + ky:6 + ky, :
                    ]
                    for m in range(2):
                        corner_out[t, index, 12 + row + m:13 + row + m, :] = S[
                            ALONG[1][n] * WX + 2 + kx + m, 4 + ky + k:5 + ky + k, :
                        ]

            @pl.when(has_corner(dx, dy))
            def _():
                corner_copy(t, index, index).start()

    def send_face(t, axis, side, part):
        n, tg, z = NORMAL[axis]
        vn, vt, vz = VELOCITY[axis]
        s = functools.partial(get_s, axis)
        v = functools.partial(get_v, axis)
        if part == 0:
            if side > 0:
                tiles = [s(n, 7), s(tg, 6), s(tg, 7), s(z, 6), s(z, 7)]
            else:
                tiles = [s(n, 0), s(n, 1), s(tg, 0), s(z, 0)]
            start = 2
            if t == 0:
                start = 0
                k = 6 if side > 0 else 0
                tiles = [get_a(axis, k), get_a(axis, k + 1)] + tiles
        elif side > 0:
            tiles = [v(vn, 6), v(vn, 7), v(vt, 7), v(vz, 7)]
            start = 7
        else:
            tiles = [v(vn, 0), v(vt, 0), v(vt, 1), v(vz, 0), v(vz, 1)]
            start = 6
        for index, tile in enumerate(tiles):
            face_out[t, axis, (side + 1) // 2, start + index] = tile

        @pl.when(has(axis, side))
        def _():
            face_copy(t, axis, side, side, part).start()

    def partial_velocity(layers):
        for i in layers:
            sx = functools.partial(along_x, S)
            sy = functools.partial(along_y, S)
            here = lambda c: S[c * WX + 2 + i, 4:12, :]
            accel = (
                forward_of(sx(XX, i)) + backward_of(sy(XY, i)) + backward_z(here(XZ)),
                backward_of(sx(XY, i)) + forward_of(sy(YY, i)) + backward_z(here(YZ)),
                backward_of(sx(XZ, i)) + backward_of(sy(YZ, i)) + forward_z(here(ZZ)),
            )
            for c in range(3):
                V[c * WX + 2 + i, 4:12, :] = (
                    D[i] * V[c * WX + 2 + i, 4:12, :] + A[i] * accel[c]
                )

    def receive(t):
        for axis, side in FACES:
            @pl.when(has(axis, side))
            def _():
                for part in range(2):
                    face_copy(t, axis, -side, side, part).wait_recv()
        for index, (dx, dy) in enumerate(CORNERS):
            @pl.when(has_corner(dx, dy))
            def _():
                corner_copy(t, 3 - index, index).wait_recv()

    def finish_velocity(t):
        for index, (dx, dy) in enumerate(CORNERS):
            for axis, side, other in ((0, dx, dy), (1, dy, dx)):
                at = 2 if other < 0 else 12
                for n in range(6):
                    row = axis * 12 + n * 2
                    strips[(axis * 2 + (side + 1) // 2) * 6 + n, at:at + 2, :] = (
                        corner_in[t, index, row:row + 2, :]
                    )
        for axis in range(2):
            n, tg, z = NORMAL[axis]
            vn, vt, vz = VELOCITY[axis]
            s = functools.partial(get_s, axis)
            a = functools.partial(get_a, axis)

            def add(c, k, value):
                set_v(axis, c, k, get_v(axis, c, k) + a(k) * value)

            def strip(side, m, k):
                return along_rows(strips, (axis * 2 + side) * 6 + m * 2 + k)

            lo = lambda m: face_in[t, axis, 0, 2 + m]
            hi = lambda m: face_in[t, axis, 1, 2 + m]
            a_lo = lambda k: face_in[0, axis, 0, k]
            a_hi = lambda k: face_in[0, axis, 1, k]

            set_v(axis, vn, -2, lo(5) + a_lo(0) * (
                C2 * s(n, 0) + backward_of(strip(0, 0, 0))))
            set_v(axis, vn, -1, lo(6) + a_lo(1) * (
                C1 * s(n, 0) + C2 * s(n, 1) + backward_of(strip(0, 0, 1))))
            set_v(axis, vt, -1, lo(7) + a_lo(1) * (
                C2 * s(tg, 0) + forward_of(strip(0, 1, 1))))
            set_v(axis, vz, -1, lo(8) + a_lo(1) * (
                C2 * s(z, 0) + backward_of(strip(0, 2, 1))))
            set_v(axis, vn, 8, hi(4) + a_hi(0) * (
                -C2 * s(n, 7) + backward_of(strip(1, 0, 0))))
            set_v(axis, vt, 8, hi(5) + a_hi(0) * (
                -C1 * s(tg, 7) - C2 * s(tg, 6) + forward_of(strip(1, 1, 0))))
            set_v(axis, vt, 9, hi(6) + a_hi(1) * (
                -C2 * s(tg, 7) + forward_of(strip(1, 1, 1))))
            set_v(axis, vz, 8, hi(7) + a_hi(0) * (
                -C1 * s(z, 7) - C2 * s(z, 6) + backward_of(strip(1, 2, 0))))
            set_v(axis, vz, 9, hi(8) + a_hi(1) * (
                -C2 * s(z, 7) + backward_of(strip(1, 2, 1))))

            add(vn, 0, -C2 * lo(0))
            add(vn, 6, C2 * hi(0))
            add(vn, 7, C1 * hi(0) + C2 * hi(1))
            for c, m, h in ((vt, 1, 2), (vz, 3, 3)):
                add(c, 0, -C1 * lo(m + 1) - C2 * lo(m))
                add(c, 1, -C2 * lo(m + 1))
                add(c, 7, C2 * hi(h))

    def plastic(last):
        @functools.partial(lax.fori_loop, 0, B, init_val=None, unroll=2)
        def _(i, _carry):
            vx = functools.partial(along_x, V)
            vy = functools.partial(along_y, V)
            here = lambda c: V[c * WX + 2 + i, 4:12, :]
            xx = backward_of(vx(0, i))
            yy = backward_of(vy(1, i))
            zz = backward_z(here(2))
            trace = xx + yy + zz
            third = trace * (1.0 / 3.0)
            g = shear[i]
            h = 0.5 * g
            move = (
                g * (xx - third), g * (yy - third), g * (zz - third),
                h * (forward_of(vy(0, i)) + forward_of(vx(1, i))),
                h * (forward_z(here(0)) + forward_of(vx(2, i))),
                h * (forward_z(here(1)) + forward_of(vy(2, i))),
            )
            pressure = mean[i] + bulk[i] * trace
            mean[i] = pressure
            total = [None] * 6
            for k in range(SURF):
                trial = [surf[k, c, i] + move[c] for c in range(6)]
                sq = [f * f for f in trial]
                size2 = 0.5 * (sq[0] + sq[1] + sq[2]) + (sq[3] + sq[4] + sq[5])
                lim = limit[k, i]
                factor = lim * lax.rsqrt(jnp.maximum(size2, lim * lim))
                for c in range(6):
                    new = trial[c] * factor
                    if not last:
                        surf[k, c, i] = new
                    total[c] = new if k == 0 else total[c] + new
            for c in range(6):
                value = total[c] + pressure if c < 3 else total[c]
                if last:
                    stress_out[c, i] = value
                else:
                    S[c * WX + 2 + i, 4:12, :] = value

    for load in surface_loads:
        load.wait()

    @pl.loop(0, B)
    def _(i):
        for c in range(6):
            total = surf[0, c, i]
            for k in range(1, SURF):
                total = total + surf[k, c, i]
            S[c * WX + 2 + i, 4:12, :] = total + mean[i] if c < 3 else total

    count = sum(there.astype(jnp.int32) for _, there in neighbours)
    pl.semaphore_wait(barrier, count)

    for t in range(ITERS):
        send_corners(t)
        for axis, side in FACES:
            send_face(t, axis, side, 0)
        partial_velocity((0, 1, 6, 7))
        send_face(t, 0, -1, 1)
        send_face(t, 0, 1, 1)
        partial_velocity((2, 3, 4, 5))
        send_face(t, 1, -1, 1)
        send_face(t, 1, 1, 1)
        receive(t)
        finish_velocity(t)
        plastic(t == ITERS - 1)

    for c in range(3):
        for i in range(B):
            velocity_out[c, i] = V[c * WX + 2 + i, 4:12, :]

    for t in range(ITERS):
        for axis, side in FACES:
            @pl.when(has(axis, side))
            def _():
                for part in range(2):
                    face_copy(t, axis, side, side, part).wait_send()
        for index, (dx, dy) in enumerate(CORNERS):
            @pl.when(has_corner(dx, dy))
            def _():
                corner_copy(t, index, index).wait_send()


def body(nx, ny, velocity, surfaces, mean_stress, zone, sponge, moduli, yields):
    vmem = pl.BlockSpec(memory_space=pltpu.VMEM)
    f32 = jnp.float32
    tiles = lambda *lead: pltpu.VMEM(lead + (B, 128), f32)
    return pl.pallas_call(
        functools.partial(kernel, nx, ny),
        out_shape=(
            jax.ShapeDtypeStruct((3, B, B, 128), f32),
            jax.ShapeDtypeStruct((6, B, B, 128), f32),
        ),
        in_specs=[pl.BlockSpec(memory_space=pltpu.HBM)] * 7,
        out_specs=(vmem, vmem),
        scratch_shapes=[
            tiles(3, B),
            pltpu.VMEM((B, B, 128), jnp.int32),
            pltpu.VMEM((B, B, 128), jnp.int32),
            pltpu.SMEM((3, ZONES), f32),
            pltpu.SMEM((ZONES, SURF), f32),
            tiles(SURF, 6, B),
            tiles(B),
            pltpu.VMEM((6 * WX, WY, 128), f32),
            pltpu.VMEM((3 * WX, WY, 128), f32),
            tiles(B), tiles(B), tiles(B), tiles(B),
            tiles(SURF, B),
            pltpu.VMEM((24, WY, 128), f32),
            tiles(ITERS, 2, 2, 11),
            tiles(ITERS, 2, 2, 11),
            pltpu.VMEM((ITERS, 4, 24, 128), f32),
            pltpu.VMEM((ITERS, 4, 24, 128), f32),
            pltpu.SemaphoreType.DMA((6 + SURF,)),
            pltpu.SemaphoreType.DMA((ITERS, 2, 2, 2)),
            pltpu.SemaphoreType.DMA((ITERS, 2, 2, 2)),
            pltpu.SemaphoreType.DMA((ITERS, 4)),
            pltpu.SemaphoreType.DMA((ITERS, 4)),
        ],
        compiler_params=pltpu.CompilerParams(
            collective_id=0, has_side_effects=True, vmem_limit_bytes=32 << 20
        ),
    )(*(
        pltpu.with_memory_space_constraint(array, pltpu.HBM)
        for array in (velocity, surfaces, mean_stress, zone, sponge, moduli.T, yields)
    ))


def solution(mesh):
    return jax.shard_map(
        functools.partial(body, mesh.shape["gx"], mesh.shape["gy"]),
        mesh=mesh,
        in_specs=(
            P(None, "gx", "gy", None),
            P(None, None, "gx", "gy", None),
            P("gx", "gy", None),
            P("gx", "gy", None),
            P("gx", "gy", None),
            P(),
            P(),
        ),
        out_specs=(P(None, "gx", "gy", None), P(None, "gx", "gy", None)),
        check_vma=False,
    )
```

```python
import functools

import jax
import jax.numpy as jnp
from jax import lax
from jax.experimental import pallas as pl
from jax.experimental.pallas import tpu as pltpu
from jax.sharding import PartitionSpec as P

ITERS = 3
SURF = 8
ZONES = 8
C1 = 9.0 / 8.0
C2 = -1.0 / 24.0
DT = 0.1
SPONGE = 0.1

B = 8
WX = 12
WY = 16
XX, YY, ZZ, XY, XZ, YZ = range(6)

NORMAL = ((XX, XY, XZ), (YY, XY, YZ))
ALONG = ((XY, YY, YZ), (XY, XX, XZ))
VELOCITY = ((0, 1, 2), (1, 0, 2))

FACES = ((0, -1), (0, 1), (1, -1), (1, 1))
CORNERS = ((-1, -1), (-1, 1), (1, -1), (1, 1))
CORNER_ROWS = 16


def corner_cells(ex, ey):
    cells = set()
    for axis, side, other in ((0, ex, ey), (1, ey, ex)):
        for n, layers in enumerate(((0, 1), (1,), (1,)) if side < 0 else ((0,), (0, 1), (0, 1))):
            if n == 1:
                rows = (1,) if other < 0 else (0, 1)
            else:
                rows = (0, 1) if other < 0 else (0,)
            for k in layers:
                for r in rows:
                    cells.add((ALONG[axis][n],) + ((k, r) if axis == 0 else (r, k)))
    return sorted(cells)


def kernel(
    nx, ny,
    velocity_hbm, surfaces, mean_hbm, zone_hbm, sponge_hbm, moduli_hbm, yields_hbm,
    velocity_out, stress_out,
    velocity, zone, sponge, moduli, yields, surf, mean, S, V, A, D, bulk, shear, limit, strips,
    face_out, face_in, corner_out, corner_in,
    load_sem, face_send, face_recv, corner_send, corner_recv,
):
    px, py = lax.axis_index("gx"), lax.axis_index("gy")
    f32 = jnp.float32

    small = (
        (moduli_hbm, moduli), (yields_hbm, yields), (zone_hbm, zone),
        (sponge_hbm, sponge), (mean_hbm, mean), (velocity_hbm, velocity),
    )
    loads = [
        pltpu.make_async_copy(source, target, load_sem.at[index])
        for index, (source, target) in enumerate(small)
    ]
    surface_loads = [
        pltpu.make_async_copy(surfaces.at[k], surf.at[k], load_sem.at[len(small) + k])
        for k in range(SURF)
    ]
    for load in surface_loads + loads:
        load.start()

    def has(axis, side):
        at, count = ((px, nx), (py, ny))[axis]
        return at > 0 if side < 0 else at < count - 1

    def has_corner(dx, dy):
        return jnp.logical_and(has(0, dx), has(1, dy))

    def device(dx, dy):
        return (px + dx, py + dy)

    barrier = pltpu.get_barrier_semaphore()
    neighbours = [((dx, 0), has(0, dx)) for dx in (-1, 1)]
    neighbours += [((0, dy), has(1, dy)) for dy in (-1, 1)]
    neighbours += [(d, has_corner(*d)) for d in CORNERS]
    for (dx, dy), there in neighbours:
        @pl.when(there)
        def _():
            pl.semaphore_signal(
                barrier, inc=1, device_id=device(dx, dy),
                device_id_type=pl.DeviceIdType.MESH,
            )

    zero = jnp.zeros((B, 128), f32)

    for axis, side in FACES:
        @pl.when(jnp.logical_not(has(axis, side)))
        def _():
            for t in range(ITERS):
                for tile in range(11):
                    face_in[t, axis, (side + 1) // 2, tile] = zero
    for index, (dx, dy) in enumerate(CORNERS):
        @pl.when(jnp.logical_not(has_corner(dx, dy)))
        def _():
            for t in range(ITERS):
                corner_in[t, index, 0:8, :] = zero
                corner_in[t, index, 8:16, :] = zero

    @pl.loop(0, 6 * WX)
    def _(i):
        S[i, 0:8, :] = zero
        S[i, 8:16, :] = zero

    @pl.loop(0, 24)
    def _(i):
        strips[i, 0:8, :] = zero
        strips[i, 8:16, :] = zero

    modulus = lambda z, column: moduli[column, z]
    strength = lambda z, column: yields[z, column]

    def pick(table, column, b0, b1, b2):
        v = [table(z, column) for z in range(ZONES)]
        a = [jnp.where(b0, v[2 * n + 1], v[2 * n]) for n in range(4)]
        c = [jnp.where(b1, a[2 * n + 1], a[2 * n]) for n in range(2)]
        return jnp.where(b2, c[1], c[0])

    def zone_bits(i):
        z = zone[i]
        return (z & 1) > 0, (z & 2) > 0, (z & 4) > 0

    def motion_factors():
        for i in range(B):
            damping = 1.0 - SPONGE * sponge[i].astype(f32)
            A[i] = DT * pick(modulus, 2, *zone_bits(i)) * damping
            D[i] = damping
            for c in range(3):
                V[c * WX + 2 + i, 4:12, :] = velocity[c, i]

    def yield_factors():
        @pl.loop(0, B)
        def _(i):
            bits = zone_bits(i)
            bulk[i] = DT * pick(modulus, 0, *bits)
            shear[i] = (2.0 * DT / SURF) * pick(modulus, 1, *bits)
            for k in range(SURF):
                limit[k, i] = pick(strength, k, *bits)

    lane = lax.broadcasted_iota(jnp.int32, (B, 128), 1)

    def mask(keep, value):
        return jnp.where(keep, f32(value), f32(0))

    f_up1 = mask(lane < 127, C1)
    f_up2 = mask(lane < 126, C2)
    f_dn1 = mask(lane >= 1, C2)
    b_dn1 = mask(lane >= 1, C1)
    b_up1 = mask(lane < 127, C2)
    b_dn2 = mask(lane >= 2, C2)

    def forward_z(f):
        return (
            f_up1 * pltpu.roll(f, 127, 1) - C1 * f
            + f_up2 * pltpu.roll(f, 126, 1) - f_dn1 * pltpu.roll(f, 1, 1)
        )

    def backward_z(f):
        return (
            C1 * f - b_dn1 * pltpu.roll(f, 1, 1)
            + b_up1 * pltpu.roll(f, 127, 1) - b_dn2 * pltpu.roll(f, 2, 1)
        )

    def forward_of(at):
        return C1 * (at(1) - at(0)) + C2 * (at(2) - at(-1))

    def backward_of(at):
        return C1 * (at(0) - at(-1)) + C2 * (at(1) - at(-2))

    def along_x(ref, c, i):
        return lambda o: ref[c * WX + 2 + i + o, 4:12, :]

    def along_rows(ref, n):
        return lambda o: ref[n, 4 + o:12 + o, :]

    def along_y(ref, c, i):
        return along_rows(ref, c * WX + 2 + i)

    S_rows = S.reshape(6 * WX * WY, 128)
    V_rows = V.reshape(3 * WX * WY, 128)
    A_rows = A.reshape(B * B, 128)

    def rows_of(c, k):
        return (pl.ds((c * WX + 2) * WY + 4 + k, B, stride=WY), slice(None))

    def get_s(axis, c, k):
        return S[c * WX + 2 + k, 4:12, :] if axis == 0 else S_rows[rows_of(c, k)]

    def get_v(axis, c, k):
        return V[c * WX + 2 + k, 4:12, :] if axis == 0 else V_rows[rows_of(c, k)]

    def set_v(axis, c, k, value):
        if axis == 0:
            V[c * WX + 2 + k, 4:12, :] = value
        else:
            V_rows[rows_of(c, k)] = value

    def get_a(axis, k):
        return A[k] if axis == 0 else A_rows[pl.ds(k, B, stride=B), :]

    def face_copy(t, axis, side, toward, part):
        own, other = (side + 1) // 2, (1 - side) // 2
        split = 5 if side > 0 else 4
        start, stop = (0, split) if part == 0 else (split, 9 if t else 11)
        tiles = pl.ds(start, stop - start)
        shift = (toward, 0) if axis == 0 else (0, toward)
        return pltpu.make_async_remote_copy(
            src_ref=face_out.at[t, axis, own, tiles],
            dst_ref=face_in.at[t, axis, other, tiles],
            send_sem=face_send.at[t, axis, own, part],
            recv_sem=face_recv.at[t, axis, other, part],
            device_id=device(*shift),
            device_id_type=pl.DeviceIdType.MESH,
        )

    def corner_copy(t, index, toward):
        dx, dy = CORNERS[toward]
        rows = pl.ds(0, len(corner_cells(*CORNERS[3 - index])))
        return pltpu.make_async_remote_copy(
            src_ref=corner_out.at[t, index, rows],
            dst_ref=corner_in.at[t, 3 - index, rows],
            send_sem=corner_send.at[t, index],
            recv_sem=corner_recv.at[t, 3 - index],
            device_id=device(dx, dy),
            device_id_type=pl.DeviceIdType.MESH,
        )

    def send_corners(t):
        for index, (dx, dy) in enumerate(CORNERS):
            kx, ky = (6 if dx > 0 else 0), (6 if dy > 0 else 0)
            for row, (c, x, y) in enumerate(corner_cells(-dx, -dy)):
                y_row = 4 + ky + y
                corner_out[t, index, row:row + 1, :] = S[
                    c * WX + 2 + kx + x, y_row:y_row + 1, :
                ]

            @pl.when(has_corner(dx, dy))
            def _():
                corner_copy(t, index, index).start()

    def send_face(t, axis, side, part):
        n, tg, z = NORMAL[axis]
        vn, vt, vz = VELOCITY[axis]
        s = functools.partial(get_s, axis)
        v = functools.partial(get_v, axis)
        if part == 0:
            if side > 0:
                tiles = [s(n, 7), s(tg, 6), s(tg, 7), s(z, 6), s(z, 7)]
            else:
                tiles = [s(n, 0), s(n, 1), s(tg, 0), s(z, 0)]
            start = 0
        elif side > 0:
            tiles = [v(vn, 6), v(vn, 7), v(vt, 7), v(vz, 7)]
            start = 5
        else:
            tiles = [v(vn, 0), v(vt, 0), v(vt, 1), v(vz, 0), v(vz, 1)]
            start = 4
        if part == 1 and t == 0:
            k = 6 if side > 0 else 0
            tiles += [get_a(axis, k), get_a(axis, k + 1)]
        for index, tile in enumerate(tiles):
            face_out[t, axis, (side + 1) // 2, start + index] = tile

        @pl.when(has(axis, side))
        def _():
            face_copy(t, axis, side, side, part).start()

    def partial_velocity(layers):
        for i in layers:
            sx = functools.partial(along_x, S)
            sy = functools.partial(along_y, S)
            here = lambda c: S[c * WX + 2 + i, 4:12, :]
            accel = (
                forward_of(sx(XX, i)) + backward_of(sy(XY, i)) + backward_z(here(XZ)),
                backward_of(sx(XY, i)) + forward_of(sy(YY, i)) + backward_z(here(YZ)),
                backward_of(sx(XZ, i)) + backward_of(sy(YZ, i)) + forward_z(here(ZZ)),
            )
            for c in range(3):
                V[c * WX + 2 + i, 4:12, :] = (
                    D[i] * V[c * WX + 2 + i, 4:12, :] + A[i] * accel[c]
                )

    def receive_faces(t, axis):
        for side in (-1, 1):
            @pl.when(has(axis, side))
            def _():
                for part in range(2):
                    face_copy(t, axis, -side, side, part).wait_recv()

    def receive_corners(t):
        for index, (dx, dy) in enumerate(CORNERS):
            @pl.when(has_corner(dx, dy))
            def _():
                corner_copy(t, 3 - index, index).wait_recv()

    def finish_corners(t):
        for index, (dx, dy) in enumerate(CORNERS):
            for row, (c, x, y) in enumerate(corner_cells(dx, dy)):
                cell = corner_in[t, index, row:row + 1, :]
                for axis, side, other, k, r in ((0, dx, dy, x, y), (1, dy, dx, y, x)):
                    if c in ALONG[axis]:
                        strip = (axis * 2 + (side + 1) // 2) * 6 + ALONG[axis].index(c) * 2 + k
                        at = (2 if other < 0 else 12) + r
                        strips[strip, at:at + 1, :] = cell
        for axis in range(2):
            vn, vt, vz = VELOCITY[axis]

            def add(c, side, m, k, derivative):
                at = -2 + k if side == 0 else 8 + k
                strip = along_rows(strips, (axis * 2 + side) * 6 + m * 2 + k)
                factor = face_in[0, axis, side, 9 + k]
                set_v(axis, c, at, get_v(axis, c, at) + factor * derivative(strip))

            add(vn, 0, 0, 0, backward_of)
            add(vn, 0, 0, 1, backward_of)
            add(vt, 0, 1, 1, forward_of)
            add(vz, 0, 2, 1, backward_of)
            add(vn, 1, 0, 0, backward_of)
            add(vt, 1, 1, 0, forward_of)
            add(vt, 1, 1, 1, forward_of)
            add(vz, 1, 2, 0, backward_of)
            add(vz, 1, 2, 1, backward_of)

    def finish_faces(t, axis):
        n, tg, z = NORMAL[axis]
        vn, vt, vz = VELOCITY[axis]
        s = functools.partial(get_s, axis)
        a = functools.partial(get_a, axis)

        def add(c, k, value):
            set_v(axis, c, k, get_v(axis, c, k) + a(k) * value)

        lo = lambda m: face_in[t, axis, 0, m]
        hi = lambda m: face_in[t, axis, 1, m]
        a_lo = lambda k: face_in[0, axis, 0, 9 + k]
        a_hi = lambda k: face_in[0, axis, 1, 9 + k]

        set_v(axis, vn, -2, lo(5) + a_lo(0) * (C2 * s(n, 0)))
        set_v(axis, vn, -1, lo(6) + a_lo(1) * (C1 * s(n, 0) + C2 * s(n, 1)))
        set_v(axis, vt, -1, lo(7) + a_lo(1) * (C2 * s(tg, 0)))
        set_v(axis, vz, -1, lo(8) + a_lo(1) * (C2 * s(z, 0)))
        set_v(axis, vn, 8, hi(4) + a_hi(0) * (-C2 * s(n, 7)))
        set_v(axis, vt, 8, hi(5) + a_hi(0) * (-C1 * s(tg, 7) - C2 * s(tg, 6)))
        set_v(axis, vt, 9, hi(6) + a_hi(1) * (-C2 * s(tg, 7)))
        set_v(axis, vz, 8, hi(7) + a_hi(0) * (-C1 * s(z, 7) - C2 * s(z, 6)))
        set_v(axis, vz, 9, hi(8) + a_hi(1) * (-C2 * s(z, 7)))

        add(vn, 0, -C2 * lo(0))
        add(vn, 6, C2 * hi(0))
        add(vn, 7, C1 * hi(0) + C2 * hi(1))
        for c, m, h in ((vt, 1, 2), (vz, 3, 3)):
            add(c, 0, -C1 * lo(m + 1) - C2 * lo(m))
            add(c, 1, -C2 * lo(m + 1))
            add(c, 7, C2 * hi(h))

    def plastic(last, layers):
        for i in layers:
            vx = functools.partial(along_x, V)
            vy = functools.partial(along_y, V)
            here = lambda c: V[c * WX + 2 + i, 4:12, :]
            xx = backward_of(vx(0, i))
            yy = backward_of(vy(1, i))
            zz = backward_z(here(2))
            trace = xx + yy + zz
            third = trace * (1.0 / 3.0)
            g = shear[i]
            h = 0.5 * g
            move = (
                g * (xx - third), g * (yy - third), g * (zz - third),
                h * (forward_of(vy(0, i)) + forward_of(vx(1, i))),
                h * (forward_z(here(0)) + forward_of(vx(2, i))),
                h * (forward_z(here(1)) + forward_of(vy(2, i))),
            )
            pressure = mean[i] + bulk[i] * trace
            mean[i] = pressure
            total = [None] * 6
            for k in range(SURF):
                trial = [surf[k, c, i] + move[c] for c in range(6)]
                sq = [f * f for f in trial]
                size2 = 0.5 * (sq[0] + sq[1] + sq[2]) + (sq[3] + sq[4] + sq[5])
                lim = limit[k, i]
                factor = lim * lax.rsqrt(jnp.maximum(size2, lim * lim))
                for c in range(6):
                    new = trial[c] * factor
                    if not last:
                        surf[k, c, i] = new
                    total[c] = new if k == 0 else total[c] + new
            for c in range(6):
                value = total[c] + pressure if c < 3 else total[c]
                if last:
                    stress_out[c, i] = value
                else:
                    S[c * WX + 2 + i, 4:12, :] = value
            if last:
                for c in range(3):
                    velocity_out[c, i] = here(c)

    for load in surface_loads + loads:
        load.wait()

    @functools.partial(lax.fori_loop, 0, B, init_val=None, unroll=2)
    def _(i, _carry):
        for c in range(6):
            total = surf[0, c, i]
            for k in range(1, SURF):
                total = total + surf[k, c, i]
            S[c * WX + 2 + i, 4:12, :] = total + mean[i] if c < 3 else total

    count = sum(there.astype(jnp.int32) for _, there in neighbours)
    pl.semaphore_wait(barrier, count)

    for t in range(ITERS):
        send_corners(t)
        for axis, side in FACES:
            send_face(t, axis, side, 0)
        if t == 0:
            motion_factors()
        partial_velocity((0, 1, 6, 7))
        send_face(t, 0, -1, 1)
        send_face(t, 0, 1, 1)
        partial_velocity((2, 3, 4, 5))
        send_face(t, 1, -1, 1)
        send_face(t, 1, 1, 1)
        if t == 0:
            yield_factors()
        last = t == ITERS - 1
        receive_faces(t, 1)
        finish_faces(t, 1)
        plastic(last, (3, 4))
        receive_faces(t, 0)
        finish_faces(t, 0)
        receive_corners(t)
        finish_corners(t)

        @pl.loop(0, 3)
        def _(j):
            plastic(last, (j, j + 5))

    for t in range(ITERS):
        for axis, side in FACES:
            @pl.when(has(axis, side))
            def _():
                for part in range(2):
                    face_copy(t, axis, side, side, part).wait_send()
        for index, (dx, dy) in enumerate(CORNERS):
            @pl.when(has_corner(dx, dy))
            def _():
                corner_copy(t, index, index).wait_send()


def body(nx, ny, velocity, surfaces, mean_stress, zone, sponge, moduli, yields):
    vmem = pl.BlockSpec(memory_space=pltpu.VMEM)
    f32 = jnp.float32
    tiles = lambda *lead: pltpu.VMEM(lead + (B, 128), f32)
    return pl.pallas_call(
        functools.partial(kernel, nx, ny),
        out_shape=(
            jax.ShapeDtypeStruct((3, B, B, 128), f32),
            jax.ShapeDtypeStruct((6, B, B, 128), f32),
        ),
        in_specs=[pl.BlockSpec(memory_space=pltpu.HBM)] * 7,
        out_specs=(vmem, vmem),
        scratch_shapes=[
            tiles(3, B),
            pltpu.VMEM((B, B, 128), jnp.int32),
            pltpu.VMEM((B, B, 128), jnp.int32),
            pltpu.SMEM((3, ZONES), f32),
            pltpu.SMEM((ZONES, SURF), f32),
            tiles(SURF, 6, B),
            tiles(B),
            pltpu.VMEM((6 * WX, WY, 128), f32),
            pltpu.VMEM((3 * WX, WY, 128), f32),
            tiles(B), tiles(B), tiles(B), tiles(B),
            tiles(SURF, B),
            pltpu.VMEM((24, WY, 128), f32),
            tiles(ITERS, 2, 2, 11),
            tiles(ITERS, 2, 2, 11),
            pltpu.VMEM((ITERS, 4, CORNER_ROWS, 128), f32),
            pltpu.VMEM((ITERS, 4, CORNER_ROWS, 128), f32),
            pltpu.SemaphoreType.DMA((6 + SURF,)),
            pltpu.SemaphoreType.DMA((ITERS, 2, 2, 2)),
            pltpu.SemaphoreType.DMA((ITERS, 2, 2, 2)),
            pltpu.SemaphoreType.DMA((ITERS, 4)),
            pltpu.SemaphoreType.DMA((ITERS, 4)),
        ],
        compiler_params=pltpu.CompilerParams(
            collective_id=0, has_side_effects=True, vmem_limit_bytes=32 << 20
        ),
    )(*(
        pltpu.with_memory_space_constraint(array, pltpu.HBM)
        for array in (velocity, surfaces, mean_stress, zone, sponge, moduli.T, yields)
    ))


def solution(mesh):
    return jax.shard_map(
        functools.partial(body, mesh.shape["gx"], mesh.shape["gy"]),
        mesh=mesh,
        in_specs=(
            P(None, "gx", "gy", None),
            P(None, None, "gx", "gy", None),
            P("gx", "gy", None),
            P("gx", "gy", None),
            P("gx", "gy", None),
            P(),
            P(),
        ),
        out_specs=(P(None, "gx", "gy", None), P(None, "gx", "gy", None)),
        check_vma=False,
    )
```

```python
import functools

import jax
import jax.numpy as jnp
from jax import lax
from jax.experimental import pallas as pl
from jax.experimental.pallas import tpu as pltpu
from jax.sharding import PartitionSpec as P

ITERS = 3
SURF = 8
ZONES = 8
C1 = 9.0 / 8.0
C2 = -1.0 / 24.0
DT = 0.1
SPONGE = 0.1

B = 8
WX = 12
WY = 16
XX, YY, ZZ, XY, XZ, YZ = range(6)

NORMAL = ((XX, XY, XZ), (YY, XY, YZ))
ALONG = ((XY, YY, YZ), (XY, XX, XZ))
VELOCITY = ((0, 1, 2), (1, 0, 2))

FACES = ((0, -1), (0, 1), (1, -1), (1, 1))
CORNERS = ((-1, -1), (-1, 1), (1, -1), (1, 1))
CORNER_ROWS = 16


def corner_cells(ex, ey):
    cells = set()
    for axis, side, other in ((0, ex, ey), (1, ey, ex)):
        for n, layers in enumerate(((0, 1), (1,), (1,)) if side < 0 else ((0,), (0, 1), (0, 1))):
            if n == 1:
                rows = (1,) if other < 0 else (0, 1)
            else:
                rows = (0, 1) if other < 0 else (0,)
            for k in layers:
                for r in rows:
                    cells.add((ALONG[axis][n],) + ((k, r) if axis == 0 else (r, k)))
    return sorted(cells)


def kernel(
    nx, ny,
    velocity_hbm, surfaces, mean_hbm, zone_hbm, sponge_hbm, moduli_hbm, yields_hbm,
    velocity_out, stress_out,
    velocity, zone, sponge, moduli, yields, surf, mean, S, V, A, D, bulk, shear, limit, strips,
    face_out, face_in, corner_out, corner_in,
    load_sem, face_send, face_recv, corner_send, corner_recv,
):
    px, py = lax.axis_index("gx"), lax.axis_index("gy")
    f32 = jnp.float32

    small = (
        (moduli_hbm, moduli), (yields_hbm, yields), (zone_hbm, zone),
        (sponge_hbm, sponge), (mean_hbm, mean), (velocity_hbm, velocity),
    )
    loads = [
        pltpu.make_async_copy(source, target, load_sem.at[index])
        for index, (source, target) in enumerate(small)
    ]
    surface_loads = [
        pltpu.make_async_copy(surfaces.at[k], surf.at[k], load_sem.at[len(small) + k])
        for k in range(SURF)
    ]
    for load in loads + surface_loads:
        load.start()

    def has(axis, side):
        at, count = ((px, nx), (py, ny))[axis]
        return at > 0 if side < 0 else at < count - 1

    def has_corner(dx, dy):
        return jnp.logical_and(has(0, dx), has(1, dy))

    def device(dx, dy):
        return (px + dx, py + dy)

    barrier = pltpu.get_barrier_semaphore()
    neighbours = [((dx, 0), has(0, dx)) for dx in (-1, 1)]
    neighbours += [((0, dy), has(1, dy)) for dy in (-1, 1)]
    neighbours += [(d, has_corner(*d)) for d in CORNERS]
    for (dx, dy), there in neighbours:
        @pl.when(there)
        def _():
            pl.semaphore_signal(
                barrier, inc=1, device_id=device(dx, dy),
                device_id_type=pl.DeviceIdType.MESH,
            )

    zero = jnp.zeros((B, 128), f32)

    for axis, side in FACES:
        @pl.when(jnp.logical_not(has(axis, side)))
        def _():
            for t in range(ITERS):
                for tile in range(11):
                    face_in[t, axis, (side + 1) // 2, tile] = zero
    for index, (dx, dy) in enumerate(CORNERS):
        @pl.when(jnp.logical_not(has_corner(dx, dy)))
        def _():
            for t in range(ITERS):
                corner_in[t, index, 0:8, :] = zero
                corner_in[t, index, 8:16, :] = zero

    @pl.loop(0, 6 * WX)
    def _(i):
        S[i, 0:8, :] = zero
        S[i, 8:16, :] = zero

    @pl.loop(0, 24)
    def _(i):
        strips[i, 0:8, :] = zero
        strips[i, 8:16, :] = zero

    modulus = lambda z, column: moduli[column, z]
    strength = lambda z, column: yields[z, column]

    def pick(table, column, b0, b1, b2):
        v = [table(z, column) for z in range(ZONES)]
        a = [jnp.where(b0, v[2 * n + 1], v[2 * n]) for n in range(4)]
        c = [jnp.where(b1, a[2 * n + 1], a[2 * n]) for n in range(2)]
        return jnp.where(b2, c[1], c[0])

    def zone_bits(i):
        z = zone[i]
        return (z & 1) > 0, (z & 2) > 0, (z & 4) > 0

    def motion_factors():
        for i in range(B):
            damping = 1.0 - SPONGE * sponge[i].astype(f32)
            A[i] = DT * pick(modulus, 2, *zone_bits(i)) * damping
            D[i] = damping
            for c in range(3):
                V[c * WX + 2 + i, 4:12, :] = velocity[c, i]

    def yield_factors():
        @pl.loop(0, B)
        def _(i):
            bits = zone_bits(i)
            bulk[i] = DT * pick(modulus, 0, *bits)
            shear[i] = (2.0 * DT / SURF) * pick(modulus, 1, *bits)
            for k in range(SURF):
                limit[k, i] = pick(strength, k, *bits)

    lane = lax.broadcasted_iota(jnp.int32, (B, 128), 1)

    def mask(keep, value):
        return jnp.where(keep, f32(value), f32(0))

    f_up1 = mask(lane < 127, C1)
    f_up2 = mask(lane < 126, C2)
    f_dn1 = mask(lane >= 1, C2)
    b_dn1 = mask(lane >= 1, C1)
    b_up1 = mask(lane < 127, C2)
    b_dn2 = mask(lane >= 2, C2)

    def forward_z(f):
        return (
            f_up1 * pltpu.roll(f, 127, 1) - C1 * f
            + f_up2 * pltpu.roll(f, 126, 1) - f_dn1 * pltpu.roll(f, 1, 1)
        )

    def backward_z(f):
        return (
            C1 * f - b_dn1 * pltpu.roll(f, 1, 1)
            + b_up1 * pltpu.roll(f, 127, 1) - b_dn2 * pltpu.roll(f, 2, 1)
        )

    def forward_of(at):
        return C1 * (at(1) - at(0)) + C2 * (at(2) - at(-1))

    def backward_of(at):
        return C1 * (at(0) - at(-1)) + C2 * (at(1) - at(-2))

    def along_x(ref, c, i):
        return lambda o: ref[c * WX + 2 + i + o, 4:12, :]

    def along_rows(ref, n):
        return lambda o: ref[n, 4 + o:12 + o, :]

    def along_y(ref, c, i):
        return along_rows(ref, c * WX + 2 + i)

    S_rows = S.reshape(6 * WX * WY, 128)
    V_rows = V.reshape(3 * WX * WY, 128)
    A_rows = A.reshape(B * B, 128)

    def rows_of(c, k):
        return (pl.ds((c * WX + 2) * WY + 4 + k, B, stride=WY), slice(None))

    def get_s(axis, c, k):
        return S[c * WX + 2 + k, 4:12, :] if axis == 0 else S_rows[rows_of(c, k)]

    def get_v(axis, c, k):
        return V[c * WX + 2 + k, 4:12, :] if axis == 0 else V_rows[rows_of(c, k)]

    def set_v(axis, c, k, value):
        if axis == 0:
            V[c * WX + 2 + k, 4:12, :] = value
        else:
            V_rows[rows_of(c, k)] = value

    def get_a(axis, k):
        return A[k] if axis == 0 else A_rows[pl.ds(k, B, stride=B), :]

    def face_copy(t, axis, side, toward, part):
        own, other = (side + 1) // 2, (1 - side) // 2
        split = 5 if side > 0 else 4
        start, stop = (0, split) if part == 0 else (split, 9 if t else 11)
        tiles = pl.ds(start, stop - start)
        shift = (toward, 0) if axis == 0 else (0, toward)
        return pltpu.make_async_remote_copy(
            src_ref=face_out.at[t, axis, own, tiles],
            dst_ref=face_in.at[t, axis, other, tiles],
            send_sem=face_send.at[t, axis, own, part],
            recv_sem=face_recv.at[t, axis, other, part],
            device_id=device(*shift),
            device_id_type=pl.DeviceIdType.MESH,
        )

    def corner_copy(t, index, toward):
        dx, dy = CORNERS[toward]
        rows = pl.ds(0, len(corner_cells(*CORNERS[3 - index])))
        return pltpu.make_async_remote_copy(
            src_ref=corner_out.at[t, index, rows],
            dst_ref=corner_in.at[t, 3 - index, rows],
            send_sem=corner_send.at[t, index],
            recv_sem=corner_recv.at[t, 3 - index],
            device_id=device(dx, dy),
            device_id_type=pl.DeviceIdType.MESH,
        )

    def send_corners(t):
        for index, (dx, dy) in enumerate(CORNERS):
            kx, ky = (6 if dx > 0 else 0), (6 if dy > 0 else 0)
            for row, (c, x, y) in enumerate(corner_cells(-dx, -dy)):
                y_row = 4 + ky + y
                corner_out[t, index, row:row + 1, :] = S[
                    c * WX + 2 + kx + x, y_row:y_row + 1, :
                ]

            @pl.when(has_corner(dx, dy))
            def _():
                corner_copy(t, index, index).start()

    def send_face(t, axis, side, part):
        n, tg, z = NORMAL[axis]
        vn, vt, vz = VELOCITY[axis]
        s = functools.partial(get_s, axis)
        v = functools.partial(get_v, axis)
        if part == 0:
            if side > 0:
                tiles = [s(n, 7), s(tg, 6), s(tg, 7), s(z, 6), s(z, 7)]
            else:
                tiles = [s(n, 0), s(n, 1), s(tg, 0), s(z, 0)]
            start = 0
        elif side > 0:
            tiles = [v(vn, 6), v(vn, 7), v(vt, 7), v(vz, 7)]
            start = 5
        else:
            tiles = [v(vn, 0), v(vt, 0), v(vt, 1), v(vz, 0), v(vz, 1)]
            start = 4
        if part == 1 and t == 0:
            k = 6 if side > 0 else 0
            tiles += [get_a(axis, k), get_a(axis, k + 1)]
        for index, tile in enumerate(tiles):
            face_out[t, axis, (side + 1) // 2, start + index] = tile

        @pl.when(has(axis, side))
        def _():
            face_copy(t, axis, side, side, part).start()

    def partial_velocity(layers):
        for i in layers:
            sx = functools.partial(along_x, S)
            sy = functools.partial(along_y, S)
            here = lambda c: S[c * WX + 2 + i, 4:12, :]
            accel = (
                forward_of(sx(XX, i)) + backward_of(sy(XY, i)) + backward_z(here(XZ)),
                backward_of(sx(XY, i)) + forward_of(sy(YY, i)) + backward_z(here(YZ)),
                backward_of(sx(XZ, i)) + backward_of(sy(YZ, i)) + forward_z(here(ZZ)),
            )
            for c in range(3):
                V[c * WX + 2 + i, 4:12, :] = (
                    D[i] * V[c * WX + 2 + i, 4:12, :] + A[i] * accel[c]
                )

    def receive_faces(t, axis):
        for side in (-1, 1):
            @pl.when(has(axis, side))
            def _():
                for part in range(2):
                    face_copy(t, axis, -side, side, part).wait_recv()

    def receive_corners(t):
        for index, (dx, dy) in enumerate(CORNERS):
            @pl.when(has_corner(dx, dy))
            def _():
                corner_copy(t, 3 - index, index).wait_recv()

    def finish_corners(t):
        for index, (dx, dy) in enumerate(CORNERS):
            for row, (c, x, y) in enumerate(corner_cells(dx, dy)):
                cell = corner_in[t, index, row:row + 1, :]
                for axis, side, other, k, r in ((0, dx, dy, x, y), (1, dy, dx, y, x)):
                    if c in ALONG[axis]:
                        strip = (axis * 2 + (side + 1) // 2) * 6 + ALONG[axis].index(c) * 2 + k
                        at = (2 if other < 0 else 12) + r
                        strips[strip, at:at + 1, :] = cell
        for axis in range(2):
            vn, vt, vz = VELOCITY[axis]

            def add(c, side, m, k, derivative):
                at = -2 + k if side == 0 else 8 + k
                strip = along_rows(strips, (axis * 2 + side) * 6 + m * 2 + k)
                factor = face_in[0, axis, side, 9 + k]
                set_v(axis, c, at, get_v(axis, c, at) + factor * derivative(strip))

            add(vn, 0, 0, 0, backward_of)
            add(vn, 0, 0, 1, backward_of)
            add(vt, 0, 1, 1, forward_of)
            add(vz, 0, 2, 1, backward_of)
            add(vn, 1, 0, 0, backward_of)
            add(vt, 1, 1, 0, forward_of)
            add(vt, 1, 1, 1, forward_of)
            add(vz, 1, 2, 0, backward_of)
            add(vz, 1, 2, 1, backward_of)

    def finish_faces(t, axis):
        n, tg, z = NORMAL[axis]
        vn, vt, vz = VELOCITY[axis]
        s = functools.partial(get_s, axis)
        a = functools.partial(get_a, axis)

        def add(c, k, value):
            set_v(axis, c, k, get_v(axis, c, k) + a(k) * value)

        lo = lambda m: face_in[t, axis, 0, m]
        hi = lambda m: face_in[t, axis, 1, m]
        a_lo = lambda k: face_in[0, axis, 0, 9 + k]
        a_hi = lambda k: face_in[0, axis, 1, 9 + k]

        set_v(axis, vn, -2, lo(5) + a_lo(0) * (C2 * s(n, 0)))
        set_v(axis, vn, -1, lo(6) + a_lo(1) * (C1 * s(n, 0) + C2 * s(n, 1)))
        set_v(axis, vt, -1, lo(7) + a_lo(1) * (C2 * s(tg, 0)))
        set_v(axis, vz, -1, lo(8) + a_lo(1) * (C2 * s(z, 0)))
        set_v(axis, vn, 8, hi(4) + a_hi(0) * (-C2 * s(n, 7)))
        set_v(axis, vt, 8, hi(5) + a_hi(0) * (-C1 * s(tg, 7) - C2 * s(tg, 6)))
        set_v(axis, vt, 9, hi(6) + a_hi(1) * (-C2 * s(tg, 7)))
        set_v(axis, vz, 8, hi(7) + a_hi(0) * (-C1 * s(z, 7) - C2 * s(z, 6)))
        set_v(axis, vz, 9, hi(8) + a_hi(1) * (-C2 * s(z, 7)))

        add(vn, 0, -C2 * lo(0))
        add(vn, 6, C2 * hi(0))
        add(vn, 7, C1 * hi(0) + C2 * hi(1))
        for c, m, h in ((vt, 1, 2), (vz, 3, 3)):
            add(c, 0, -C1 * lo(m + 1) - C2 * lo(m))
            add(c, 1, -C2 * lo(m + 1))
            add(c, 7, C2 * hi(h))

    def plastic(last, layers):
        for i in layers:
            vx = functools.partial(along_x, V)
            vy = functools.partial(along_y, V)
            here = lambda c: V[c * WX + 2 + i, 4:12, :]
            xx = backward_of(vx(0, i))
            yy = backward_of(vy(1, i))
            zz = backward_z(here(2))
            trace = xx + yy + zz
            third = trace * (1.0 / 3.0)
            g = shear[i]
            h = 0.5 * g
            move = (
                g * (xx - third), g * (yy - third), g * (zz - third),
                h * (forward_of(vy(0, i)) + forward_of(vx(1, i))),
                h * (forward_z(here(0)) + forward_of(vx(2, i))),
                h * (forward_z(here(1)) + forward_of(vy(2, i))),
            )
            pressure = mean[i] + bulk[i] * trace
            mean[i] = pressure
            total = [None] * 6
            for k in range(SURF):
                trial = [surf[k, c, i] + move[c] for c in range(6)]
                sq = [f * f for f in trial]
                size2 = 0.5 * (sq[0] + sq[1] + sq[2]) + (sq[3] + sq[4] + sq[5])
                lim = limit[k, i]
                factor = lim * lax.rsqrt(jnp.maximum(size2, lim * lim))
                for c in range(6):
                    new = trial[c] * factor
                    if not last:
                        surf[k, c, i] = new
                    total[c] = new if k == 0 else total[c] + new
            for c in range(6):
                value = total[c] + pressure if c < 3 else total[c]
                if last:
                    stress_out[c, i] = value
                else:
                    S[c * WX + 2 + i, 4:12, :] = value
            if last:
                for c in range(3):
                    velocity_out[c, i] = here(c)

    for load in loads:
        load.wait()
    motion_factors()
    for load in surface_loads:
        load.wait()

    @functools.partial(lax.fori_loop, 0, B, init_val=None, unroll=2)
    def _(i, _carry):
        for c in range(6):
            total = surf[0, c, i]
            for k in range(1, SURF):
                total = total + surf[k, c, i]
            S[c * WX + 2 + i, 4:12, :] = total + mean[i] if c < 3 else total

    count = sum(there.astype(jnp.int32) for _, there in neighbours)
    pl.semaphore_wait(barrier, count)

    for t in range(ITERS):
        send_corners(t)
        send_face(t, 0, -1, 0)
        send_face(t, 0, 1, 0)
        partial_velocity((0, 1, 6, 7))
        send_face(t, 0, -1, 1)
        send_face(t, 0, 1, 1)
        send_face(t, 1, -1, 0)
        send_face(t, 1, 1, 0)
        partial_velocity((2, 3, 4, 5))
        send_face(t, 1, -1, 1)
        send_face(t, 1, 1, 1)
        if t == 0:
            yield_factors()
        last = t == ITERS - 1
        receive_faces(t, 1)
        finish_faces(t, 1)
        plastic(last, (3, 4))
        receive_faces(t, 0)
        finish_faces(t, 0)
        receive_corners(t)
        finish_corners(t)

        @pl.loop(0, 3)
        def _(j):
            plastic(last, (j, j + 5))

    for t in range(ITERS):
        for axis, side in FACES:
            @pl.when(has(axis, side))
            def _():
                for part in range(2):
                    face_copy(t, axis, side, side, part).wait_send()
        for index, (dx, dy) in enumerate(CORNERS):
            @pl.when(has_corner(dx, dy))
            def _():
                corner_copy(t, index, index).wait_send()


def body(nx, ny, velocity, surfaces, mean_stress, zone, sponge, moduli, yields):
    vmem = pl.BlockSpec(memory_space=pltpu.VMEM)
    f32 = jnp.float32
    tiles = lambda *lead: pltpu.VMEM(lead + (B, 128), f32)
    return pl.pallas_call(
        functools.partial(kernel, nx, ny),
        out_shape=(
            jax.ShapeDtypeStruct((3, B, B, 128), f32),
            jax.ShapeDtypeStruct((6, B, B, 128), f32),
        ),
        in_specs=[pl.BlockSpec(memory_space=pltpu.HBM)] * 7,
        out_specs=(vmem, vmem),
        scratch_shapes=[
            tiles(3, B),
            pltpu.VMEM((B, B, 128), jnp.int32),
            pltpu.VMEM((B, B, 128), jnp.int32),
            pltpu.SMEM((3, ZONES), f32),
            pltpu.SMEM((ZONES, SURF), f32),
            tiles(SURF, 6, B),
            tiles(B),
            pltpu.VMEM((6 * WX, WY, 128), f32),
            pltpu.VMEM((3 * WX, WY, 128), f32),
            tiles(B), tiles(B), tiles(B), tiles(B),
            tiles(SURF, B),
            pltpu.VMEM((24, WY, 128), f32),
            tiles(ITERS, 2, 2, 11),
            tiles(ITERS, 2, 2, 11),
            pltpu.VMEM((ITERS, 4, CORNER_ROWS, 128), f32),
            pltpu.VMEM((ITERS, 4, CORNER_ROWS, 128), f32),
            pltpu.SemaphoreType.DMA((6 + SURF,)),
            pltpu.SemaphoreType.DMA((ITERS, 2, 2, 2)),
            pltpu.SemaphoreType.DMA((ITERS, 2, 2, 2)),
            pltpu.SemaphoreType.DMA((ITERS, 4)),
            pltpu.SemaphoreType.DMA((ITERS, 4)),
        ],
        compiler_params=pltpu.CompilerParams(
            collective_id=0, has_side_effects=True, vmem_limit_bytes=32 << 20
        ),
    )(*(
        pltpu.with_memory_space_constraint(array, pltpu.HBM)
        for array in (velocity, surfaces, mean_stress, zone, sponge, moduli.T, yields)
    ))


def solution(mesh):
    return jax.shard_map(
        functools.partial(body, mesh.shape["gx"], mesh.shape["gy"]),
        mesh=mesh,
        in_specs=(
            P(None, "gx", "gy", None),
            P(None, None, "gx", "gy", None),
            P("gx", "gy", None),
            P("gx", "gy", None),
            P("gx", "gy", None),
            P(),
            P(),
        ),
        out_specs=(P(None, "gx", "gy", None), P(None, "gx", "gy", None)),
        check_vma=False,
    )
```
